128 devices in a mesh: row: 16 (over y, z), col: 8 (over x, core).
Axes of the slice: x: 4, y: 4, z: 4, core: 2. Of those that a mesh axis runs over, the one named last changes fastest.
Arguments:
- descriptors: bfloat16 [131072, 512], P(('row', 'col')), may hold values from -6 to 6
- center_index: int32 [16384], replicated, may hold values from 0 to 131071, as said below
- panel_index: int32 [1], replicated, may hold values from 0 to 15
Outputs:
- schur: float32 [16384, 16384], P('row', 'col')
- panel_factor: float32 [16384, 1024], P('row', 'col')
The draws below stay inside these ranges and needn't reach their ends.
Inputs may be any that keep to these rules, and one draw needn't show every extreme that they name: Center j is row center_index[j] mod 1024 of shard center_index[j] // 1024, shards numbered row-major over row and col. In each aligned run of 128 centers no shard supplies more than 4 centers, and some shard supplies exactly 4.
All inputs are finite; a program needn't handle non-finite values.
Results may differ from the reference program's by a relative error of at most 0.0003.
Values may be sent and summed in bfloat16 or wider, within the bound.
No kernel may reach another device: no remote copies, remote signals or barrier semaphores. Data moves between devices by JAX's collectives and lax.ppermute only.
A program may use at most 128 MiB of HBM per device.

```python
import jax
import jax.numpy as jnp
from jax import lax

D = 512
PANEL = 1024
GROUP = 128
DATA_DEV = 1024
CAP = 4
CENTERS = 16384
TILE_ROWS = 1024
NDATA = 131072
N_ROW = 16
N_COL = 8
DEVICES = 128


def draw_center_index(key, part):
    key_hot, key_order, key_count, key_row = jax.random.split(key, 4)
    groups = CENTERS // GROUP
    hot_sources = jax.random.permutation(key_hot, DEVICES)[:max(1, DEVICES // 8)]
    is_hot = jnp.zeros((DEVICES,), jnp.int32).at[hot_sources].set(1)
    jitter = jax.random.randint(key_order, (groups, DEVICES), 0, DEVICES)
    scores = (jitter + is_hot[None, :] * DEVICES) * DEVICES + jnp.arange(DEVICES, dtype=jnp.int32)[None, :]
    source_order = jnp.argsort(-scores, axis=1, stable=True).astype(jnp.int32)
    lowest = (GROUP + DEVICES - 1) // DEVICES
    counts = jax.random.randint(key_count, (groups, DEVICES), lowest, CAP + 1)
    counts = jnp.where(jnp.take(is_hot, source_order) == 1, CAP, counts)
    counts = counts.at[:, 0].set(CAP)
    block_ends = jnp.cumsum(counts, axis=1)
    positions = jnp.arange(GROUP, dtype=jnp.int32)
    block_of = jnp.sum((block_ends[:, None, :] <= positions[None, :, None]).astype(jnp.int32), axis=2)
    source = jnp.take_along_axis(source_order, block_of, axis=1)
    row_in_shard = jax.random.randint(key_row, (groups, GROUP), 0, DATA_DEV)
    return (source * DATA_DEV + row_in_shard).reshape(-1).astype(jnp.int32)


def level_of(rng, shape, cuts, low, largest):
    loudness, own = 1.0, jax.random.fold_in(rng, 6)
    for axis_at, parts in cuts:
        draws = jnp.exp(jax.random.uniform(jax.random.fold_in(own, axis_at), (parts,), jnp.float32, low / len(cuts), largest / len(cuts)))
        loudness = loudness * jnp.repeat(draws, shape[axis_at] // parts).reshape([-1 if axis == axis_at else 1 for axis in range(len(shape))])
    return loudness


def centred(key, shape, spread, limit, cuts=(), held_as=jnp.bfloat16):
    factor_of = level_of(key, shape, cuts, -0.22, 0.18) if cuts else 1.0
    result = jax.random.normal(key, shape, jnp.float32) * spread * factor_of
    return jnp.minimum(jnp.maximum(result, -limit), limit).astype(held_as)


def setup_inputs(seed: int = 0) -> dict:
    splits = jax.random.split(jax.random.key(seed), 4)
    descriptors = centred(splits[0], (NDATA, D), 1.0, 6.0, ((0, 128),))
    center_index = draw_center_index(jax.random.fold_in(splits[3], 71), 0)
    panel_index = jax.random.randint(splits[2], (1,), 0, CENTERS // PANEL).astype(jnp.int32)
    return {"descriptors": descriptors, "center_index": center_index, "panel_index": panel_index}


ridge = 1.0

def gram_block(left, right, left_sq, right_sq):
    inner = lax.dot_general(left.astype(jnp.float32), right.astype(jnp.float32), (((1,), (1,)), ((), ())), preferred_element_type=jnp.float32)
    return jnp.exp(-(left_sq[:, None] + right_sq[None, :] - 2.0 * inner) / D)

def reference(descriptors, center_index, panel_index):
    centers = jnp.take(descriptors, center_index.astype(jnp.int32), axis=0)
    sq_norm = jnp.sum(jnp.square(centers.astype(jnp.float32)), axis=1)
    start_pos = (panel_index[0] * PANEL).astype(jnp.int32)
    panel_centers = lax.dynamic_slice_in_dim(centers, start_pos, PANEL, 0)
    panel_sq = lax.dynamic_slice_in_dim(sq_norm, start_pos, PANEL, 0)
    positions = jnp.arange(CENTERS, dtype=jnp.int32)
    panel_pos = start_pos + jnp.arange(PANEL, dtype=jnp.int32)
    diag_block = gram_block(panel_centers, panel_centers, panel_sq, panel_sq) + ridge * jnp.eye(PANEL, dtype=jnp.float32)
    diag_factor = jnp.linalg.cholesky(diag_block)
    all_block = gram_block(centers, panel_centers, sq_norm, panel_sq)
    all_block = all_block + ridge * (positions[:, None] == panel_pos[None, :]).astype(jnp.float32)
    panel_factor = lax.linalg.triangular_solve(diag_factor, all_block, left_side=False, lower=True, transpose_a=True)
    stored = ((jnp.arange(N_ROW, dtype=jnp.int32)[None, :, None] * N_COL + jnp.arange(N_COL, dtype=jnp.int32)[:, None, None]) * GROUP + jnp.arange(GROUP, dtype=jnp.int32)[None, None, :]).reshape(-1)
    col_centers = jnp.take(centers, stored, axis=0)
    col_sq = jnp.take(sq_norm, stored, axis=0)
    col_factor = jnp.take(panel_factor, stored, axis=0)

    def row_tile(items):
        tile_centers, tile_sq, tile_factor, tile_pos = items
        kernel = gram_block(tile_centers, col_centers, tile_sq, col_sq)
        kernel = kernel + ridge * (tile_pos[:, None] == stored[None, :]).astype(jnp.float32)
        update = lax.dot_general(tile_factor.astype(jnp.float32), col_factor.astype(jnp.float32), (((1,), (1,)), ((), ())), precision=lax.Precision.HIGHEST, preferred_element_type=jnp.float32)
        return kernel - update
    schur = lax.map(row_tile, (centers.reshape(N_ROW, TILE_ROWS, D), sq_norm.reshape(N_ROW, TILE_ROWS), panel_factor.reshape(N_ROW, TILE_ROWS, PANEL), positions.reshape(N_ROW, TILE_ROWS)))
    return (schur.reshape(CENTERS, CENTERS), panel_factor)
```

```python
import functools

import jax
import jax.numpy as jnp
from jax import lax
from jax.experimental import pallas as pl
from jax.experimental.pallas import tpu as pltpu
from jax.sharding import PartitionSpec as P

D = 512
PANEL = 1024
GROUP = 128
DATA_DEV = 1024
CAP = 4
N_ROW = 16
N_COL = 8
DEVICES = 128
RIDGE = 1.0
F32 = jnp.float32
BF = jnp.bfloat16
NT = (((1,), (1,)), ((), ()))
NN = (((1,), (0,)), ((), ()))
TN = (((0,), (0,)), ((), ()))


def dot(a, b, dims):
    return lax.dot_general(a, b, dims, preferred_element_type=F32)


def split(x):
    high = x.astype(BF)
    return high, (x - high.astype(F32)).astype(BF)


def dot3(a, b, dims):
    (ah, al), (bh, bl) = a, b
    return dot(ah, bh, dims) + (dot(ah, bl, dims) + dot(al, bh, dims))


def iota(shape, dim):
    return lax.broadcasted_iota(jnp.int32, shape, dim)


def sq_col(x):
    x = x.astype(F32)
    return jnp.sum(x * x, axis=1, keepdims=True)


def sq_row(x):
    x = x.astype(F32)
    high, low = split(x * x)
    ones = jnp.ones((8, x.shape[1]), BF)
    return (dot(ones, high, NT) + dot(ones, low, NT))[0:1]


def gram(left, right, left_sq, right_sq):
    return jnp.exp(-(left_sq + right_sq - 2.0 * dot(left, right, NT)) / D)


def send_kernel(where_ref, index_ref, desc_ref, out_ref):
    flat = where_ref[0]
    index = index_ref[...]
    match = lax.shift_right_logical(index, 10) == flat
    local = jnp.bitwise_and(index, DATA_DEV - 1).astype(F32)
    before = (iota((GROUP, GROUP), 0) < iota((GROUP, GROUP), 1)).astype(BF)
    rank = dot(match.astype(BF), before, NN)
    desc = desc_ref[...]
    rows = iota((DEVICES, DATA_DEV), 1).astype(F32)
    for k in range(CAP):
        slot = match & (rank == k)
        row = jnp.sum(jnp.where(slot, local, 0.0), axis=1, keepdims=True)
        pick = (rows == row).astype(BF)
        out_ref[:, k * D : (k + 1) * D] = dot(pick, desc, NN).astype(BF)


def take_group(index_row, arrived_ref, base):
    square = (GROUP, GROUP)
    shard_row = lax.shift_right_logical(index_row, 10).astype(F32)
    shard_row = jnp.broadcast_to(shard_row, square)
    eye = iota(square, 0) == iota(square, 1)
    shard_col = jnp.sum(jnp.where(eye, shard_row, 0.0), axis=1, keepdims=True)
    earlier = iota(square, 1) < iota(square, 0)
    rank = jnp.sum(
        jnp.where((shard_row == shard_col) & earlier, 1.0, 0.0), axis=1, keepdims=True
    )
    source = iota((GROUP, DEVICES), 1).astype(F32) == shard_col
    total = jnp.zeros((GROUP, D), F32)
    for k in range(CAP):
        pick = (source & (rank == k)).astype(BF)
        total = total + dot(pick, arrived_ref[:, (base + k) * D : (base + k + 1) * D], NN)
    return total.astype(BF)


def take_kernel(where_ref, index_ref, arrived_ref, out_ref):
    out_ref[0:GROUP] = take_group(index_ref[pl.ds(where_ref[0], 1), :], arrived_ref, 0)
    out_ref[GROUP:] = take_group(index_ref[pl.ds(where_ref[1], 1), :], arrived_ref, CAP)


def lane_b(x, c):
    return jnp.broadcast_to(x[:, c : c + 1], (8, 128))


def sub_b(x, j):
    return jnp.broadcast_to(x[j : j + 1, :], (8, 128))


def inverse_factor_128(x, sub):
    lane = iota((8, 128), 1)
    w = [(lane == sub + 8 * g).astype(F32) for g in range(16)]
    for t in range(16):
        first = 8 * t
        c = [lane_b(x[t], first + j) for j in range(8)]
        xt, wt = x[t], w[t]
        scale = jnp.zeros((8, 128), F32)
        rows = []
        for j in range(8):
            pivot = sub_b(c[j], j)
            over = 1.0 / pivot
            scale = jnp.where(sub == j, lax.rsqrt(pivot), scale)
            xj, wj = sub_b(xt, j), sub_b(wt, j)
            cj = [sub_b(c[q], j) for q in range(j + 1, 8)]
            rows.append((over, cj, xj, wj))
            if j < 7:
                m = jnp.where(sub > j, c[j] * over, 0.0)
                for q in range(j + 1, 8):
                    c[q] = c[q] - m * cj[q - j - 1]
                xt = xt - m * xj
                wt = wt - m * wj
        w[t] = wt * scale
        for g in range(t + 1, 16):
            xg, wg = x[g], w[g]
            c = [lane_b(xg, first + j) for j in range(8)]
            for j in range(8):
                over, cj, xj, wj = rows[j]
                m = c[j] * over
                for q in range(j + 1, 8):
                    c[q] = c[q] - m * cj[q - j - 1]
                xg = xg - m * xj
                wg = wg - m * wj
            x[g], w[g] = xg, wg
    return jnp.concatenate(w, 0)


def factor_kernel(panel_ref, high_ref, low_ref, x_ref):
    blocks = PANEL // 128
    panel = panel_ref[...]
    panel_row = sq_row(panel)
    panel_col = sq_col(panel)
    for i in range(blocks):
        s = slice(i * 128, i * 128 + 128)
        block = gram(panel[s], panel, panel_col[s], panel_row)
        eye = iota((128, PANEL), 1) == iota((128, PANEL), 0) + i * 128
        x_ref[s, :] = block + jnp.where(eye, RIDGE, 0.0)
    sub = iota((8, 128), 0)

    def step(k, _):
        k0 = pl.multiple_of(k * 128, 128)
        at_k = pl.ds(k0, 128)
        diag = x_ref[at_k, at_k]
        inverse = inverse_factor_128([diag[8 * g : 8 * g + 8] for g in range(16)], sub)
        x_ref[at_k, at_k] = jnp.where(iota((128, 128), 0) == iota((128, 128), 1), 1.0, 0.0)
        strip = dot3(split(inverse), split(x_ref[at_k, :]), NN)
        x_ref[at_k, :] = strip
        strip = split(strip)

        def update(i, _):
            at_i = pl.ds(pl.multiple_of(i * 128, 128), 128)
            left = split(x_ref[at_k, at_i])
            x_ref[at_i, at_k] = jnp.zeros((128, 128), F32)
            x_ref[at_i, :] -= dot3(left, strip, TN)
            return 0

        lax.fori_loop(k + 1, blocks, update, 0)
        return 0

    lax.fori_loop(0, blocks, step, 0)
    for i in range(blocks):
        s = slice(i * 128, i * 128 + 128)
        lower = iota((128, PANEL), 1) < (i + 1) * 128
        high, low = split(jnp.where(lower, x_ref[s, :], 0.0))
        high_ref[s, :] = high
        low_ref[s, :] = low


COL_TILE = 512
ROW_TILE = 256


def tile_kernel(
    where_ref, both_ref, col_ref, high_ref, low_ref, schur_ref, factor_ref, zh_ref, zl_ref
):
    my_row, my_col, owner = where_ref[0], where_ref[1], where_ref[2]
    panel = both_ref[PANEL:, :]
    panel_row = sq_row(panel)
    step = pl.program_id(0)

    @pl.when(step == 0)
    def _():
        for i in range(PANEL // ROW_TILE):
            s = slice(i * ROW_TILE, (i + 1) * ROW_TILE)
            rows = both_ref[s, :]
            block = gram(rows, panel, sq_col(rows), panel_row)
            eye = iota((ROW_TILE, PANEL), 1) == iota((ROW_TILE, PANEL), 0) + i * ROW_TILE
            block = block + jnp.where(eye & (my_row == owner), RIDGE, 0.0)
            inverse = (high_ref[...], low_ref[...])
            factor = dot3(split(block), inverse, NT)
            zh_ref[s, :], zl_ref[s, :] = split(dot3(split(factor), inverse, NN))
            share = jnp.zeros((ROW_TILE, GROUP), F32)
            for c in range(N_COL):
                share = jnp.where(my_col == c, factor[:, c * GROUP : (c + 1) * GROUP], share)
            factor_ref[s, :] = share

    cols = col_ref[...]
    at = iota((COL_TILE, PANEL), 0) + step * COL_TILE - owner * GROUP
    block = gram(cols, panel, sq_col(cols), panel_row)
    eye = (at >= 0) & (at < GROUP) & (iota((COL_TILE, PANEL), 1) == at + my_col * GROUP)
    block = split(block + jnp.where(eye, RIDGE, 0.0))
    cols_sq = sq_row(cols)
    for i in range(PANEL // ROW_TILE):
        s = slice(i * ROW_TILE, (i + 1) * ROW_TILE)
        rows = both_ref[s, :]
        tile = gram(rows, cols, sq_col(rows), cols_sq)
        shape = (ROW_TILE, COL_TILE)
        at = iota(shape, 1) + step * COL_TILE - my_row * GROUP
        eye = (at >= 0) & (at < GROUP) & (iota(shape, 0) + i * ROW_TILE == at + my_col * GROUP)
        tile = tile + jnp.where(eye, RIDGE, 0.0)
        schur_ref[s, :] = tile - dot3((zh_ref[s, :], zl_ref[s, :]), block, NT)


VMEM = pl.BlockSpec(memory_space=pltpu.VMEM)
SMEM = pl.BlockSpec(memory_space=pltpu.SMEM)


def call(kernel, out_shape, in_specs, scratch=(), **more):
    return pl.pallas_call(
        kernel,
        out_shape=out_shape,
        in_specs=in_specs,
        scratch_shapes=scratch,
        compiler_params=pltpu.CompilerParams(vmem_limit_bytes=56 << 20),
        **more,
    )


def body(descriptors, center_index, panel_index):
    my_row = lax.axis_index("row")
    my_col = lax.axis_index("col")
    owner = panel_index[0]
    flat = my_row * N_COL + my_col
    index = center_index.reshape(DEVICES, GROUP)
    sent = call(
        send_kernel, jax.ShapeDtypeStruct((DEVICES, CAP * D), BF), [SMEM, VMEM, VMEM]
    )(flat[None], index, descriptors)
    of_panel = lax.dynamic_slice_in_dim(sent, owner * N_COL, N_COL, 0)
    sent = jnp.concatenate([sent, jnp.tile(of_panel, (N_ROW, 1))], axis=1)
    arrived = lax.all_to_all(sent, ("row", "col"), 0, 0, tiled=True)
    mine = call(take_kernel, jax.ShapeDtypeStruct((2 * GROUP, D), BF), [SMEM, VMEM, VMEM])(
        jnp.stack([flat, owner * N_COL + my_col]), index, arrived
    )
    both = lax.all_gather(mine.reshape(2, GROUP, D), "col", axis=1)
    both = both.reshape(2 * PANEL, D)
    cols = lax.all_gather(mine[:GROUP], "row", axis=0, tiled=True)
    square = jax.ShapeDtypeStruct((PANEL, PANEL), BF)
    high, low = call(
        factor_kernel, (square, square), [VMEM], [pltpu.VMEM((PANEL, PANEL), F32)]
    )(both[PANEL:])
    width = N_ROW * GROUP
    schur, factor = call(
        tile_kernel,
        (
            jax.ShapeDtypeStruct((PANEL, width), F32),
            jax.ShapeDtypeStruct((PANEL, GROUP), F32),
        ),
        [SMEM, VMEM, pl.BlockSpec((COL_TILE, D), lambda i: (i, 0)), VMEM, VMEM],
        [pltpu.VMEM((PANEL, PANEL), BF), pltpu.VMEM((PANEL, PANEL), BF)],
        grid=(width // COL_TILE,),
        out_specs=(
            pl.BlockSpec((PANEL, COL_TILE), lambda i: (0, i)),
            pl.BlockSpec((PANEL, GROUP), lambda i: (0, 0)),
        ),
    )(jnp.stack([my_row, my_col, owner]), both, cols, high, low)
    return schur, factor


def solution(mesh):
    return jax.shard_map(
        body,
        mesh=mesh,
        in_specs=(P(("row", "col"), None), P(), P()),
        out_specs=(P("row", "col"), P("row", "col")),
        check_vma=False,
    )
```

```python
import functools

import jax
import jax.numpy as jnp
from jax import lax
from jax.experimental import pallas as pl
from jax.experimental.pallas import tpu as pltpu
from jax.sharding import PartitionSpec as P

D = 512
PANEL = 1024
GROUP = 128
DATA_DEV = 1024
CAP = 4
N_ROW = 16
N_COL = 8
DEVICES = 128
RIDGE = 1.0
SLOTS = 2 * CAP
F32 = jnp.float32
BF = jnp.bfloat16
NT = (((1,), (1,)), ((), ()))
NN = (((1,), (0,)), ((), ()))
TN = (((0,), (0,)), ((), ()))


def dot(a, b, dims):
    return lax.dot_general(a, b, dims, preferred_element_type=F32)


def split(x):
    high = x.astype(BF)
    return high, (x - high.astype(F32)).astype(BF)


def dot3(a, b, dims):
    (ah, al), (bh, bl) = a, b
    return dot(ah, bh, dims) + (dot(ah, bl, dims) + dot(al, bh, dims))


def iota(shape, dim):
    return lax.broadcasted_iota(jnp.int32, shape, dim)


K_EXP = 1.4426950408889634 / D


def squares(x):
    x = x.astype(F32)
    return split(x * x)


def sq_col(x):
    high, low = squares(x)
    ones = jnp.ones((x.shape[1], 128), BF)
    return (dot(high, ones, NN) + dot(low, ones, NN)) * K_EXP


def sq_row(x):
    high, low = squares(x)
    ones = jnp.ones((8, x.shape[1]), BF)
    return (dot(ones, high, NT) + dot(ones, low, NT))[0:1] * K_EXP


def widen(x, width):
    return jnp.concatenate([x] * (width // 128), 1)


def gram(left, right, left_sq, right_sq):
    inner = dot(left, right, NT)
    return jnp.exp2((inner * (2.0 * K_EXP) - widen(left_sq, right.shape[0])) - right_sq)


def send_kernel(where_ref, index_ref, desc_ref, out_ref):
    flat, first = where_ref[0], where_ref[1]
    square = (GROUP, GROUP)
    index = index_ref[...]
    match = lax.shift_right_logical(index, 10) == flat
    local = jnp.bitwise_and(index, DATA_DEV - 1).astype(F32)
    before = (iota(square, 0) < iota(square, 1)).astype(BF)
    rank = dot(match.astype(BF), before, NN)
    lane = iota(square, 1)
    own = jnp.zeros(square, F32)
    panel = jnp.zeros(square, F32)
    for k in range(CAP):
        slot = match & (rank == k)
        row = jnp.sum(jnp.where(slot, local, 0.0), axis=1, keepdims=True)
        own = jnp.where(lane == k, row, own)
        panel = jnp.where(lane == k + CAP, row, panel)
    pick = (lane == first + jnp.bitwise_and(iota(square, 0), N_COL - 1)).astype(BF)
    high, low = split(panel)
    high, low = split(own + (dot(pick, high, NN) + dot(pick, low, NN)))
    desc = desc_ref[...]
    step = 256
    for i in range(0, DEVICES * SLOTS, step):
        at = iota((step, DEVICES), 0) + i
        pick = (iota((step, DEVICES), 1) == lax.shift_right_logical(at, 3)).astype(BF)
        rows = dot(pick, high, NN) + dot(pick, low, NN)
        mine = iota((step, DEVICES), 1) == jnp.bitwise_and(at, SLOTS - 1)
        row = jnp.sum(jnp.where(mine, rows, 0.0), axis=1, keepdims=True)
        pick = (iota((step, DATA_DEV), 1).astype(F32) == row).astype(BF)
        out_ref[i : i + step] = dot(pick, desc, NN).astype(BF)


def take_group(index_row, arrived, base):
    square = (GROUP, GROUP)
    shard_row = lax.shift_right_logical(index_row, 10).astype(F32)
    shard_row = jnp.broadcast_to(shard_row, square)
    eye = iota(square, 0) == iota(square, 1)
    shard_col = jnp.sum(jnp.where(eye, shard_row, 0.0), axis=1, keepdims=True)
    earlier = iota(square, 1) < iota(square, 0)
    rank = jnp.sum(
        jnp.where((shard_row == shard_col) & earlier, 1.0, 0.0), axis=1, keepdims=True
    )
    at = shard_col * SLOTS + rank + base
    pick = (iota((GROUP, DEVICES * SLOTS), 1).astype(F32) == at).astype(BF)
    return dot(pick, arrived, NN).astype(BF)


def take_kernel(where_ref, index_ref, arrived_ref, both_ref, own_ref):
    flat, first, my_col = where_ref[0], where_ref[1], where_ref[2]
    arrived = arrived_ref[...]
    own = take_group(index_ref[pl.ds(flat, 1), :], arrived, 0)
    both_ref[0] = own
    own_ref[...] = own
    both_ref[1] = take_group(index_ref[pl.ds(first + my_col, 1), :], arrived, CAP)


def lane_b(x, c):
    return jnp.broadcast_to(x[:, c : c + 1], (8, 128))


def sub_b(x, j):
    return jnp.broadcast_to(x[j : j + 1, :], (8, 128))


def tree(terms):
    while len(terms) > 1:
        pairs = [terms[i] + terms[i + 1] for i in range(0, len(terms) - 1, 2)]
        terms = pairs + terms[len(terms) & ~1 :]
    return terms[0]


def far_update(x, w, solved, t):
    pad = jnp.zeros((8, 256), F32)
    rows = jnp.concatenate([solved, pad] if t % 2 == 0 else [pad, solved], 0)
    k = t // 2

    def place(part):
        above = [jnp.zeros((16 * k, 256), BF)] if k else []
        below = [jnp.zeros((112 - 16 * k, 256), BF)] if k < 7 else []
        return jnp.concatenate(above + [part] + below, 0)

    high, low = split(rows)
    far = jnp.concatenate(x[t + 2 :], 0)
    change = dot3(split(far), (place(high), place(low)), NN)
    for i, g in enumerate(range(t + 2, 16)):
        part = change[8 * i : 8 * i + 8]
        x[g] = x[g] - part[:, :128]
        w[g] = w[g] - part[:, 128:]


def inverse_factor_128(x, sub):
    lane = iota((8, 128), 1)
    w = [(lane == sub + 8 * g).astype(F32) for g in range(16)]
    c = [lane_b(x[0], j) for j in range(8)]
    solved = None
    for t in range(16):
        last = t == 15
        if 0 < t < 15:
            far_update(x, w, solved, t - 1)
        ahead = [] if last else [lane_b(x[t], 8 * t + 8 + q) for q in range(8)]
        xt, wt = x[t], w[t]
        out = wt
        for j in range(0, 8, 2):
            p, q, r = sub_b(c[j], j), sub_b(c[j + 1], j), sub_b(c[j + 1], j + 1)
            det = p * r - q * q
            over = 1.0 / det
            root = lax.rsqrt(p)
            over_p = root * root
            at0, at1 = sub == j, sub == j + 1
            m0 = jnp.where(at0, -1.0, jnp.where(at1, 0.0, c[j]))
            m1 = jnp.where(at1, -1.0, jnp.where(at0, 0.0, c[j + 1]))
            k0 = (m0 * r - m1 * q) * over
            k1 = (m1 * p - m0 * q) * over
            keep = jnp.logical_not(at0 | at1)

            def eliminate(v):
                return jnp.where(keep, v, 0.0) - (k0 * sub_b(v, j) + k1 * sub_b(v, j + 1))

            w0, w1 = sub_b(wt, j), sub_b(wt, j + 1)
            out = jnp.where(at0, w0 * root, out)
            out = jnp.where(at1, (w1 - (q * over_p) * w0) * lax.rsqrt(det * over_p), out)
            for i in range(j + 2, 8):
                c[i] = eliminate(c[i])
            if not last:
                ahead = [eliminate(v) for v in ahead]
                xt = eliminate(xt)
            if not last or j < 6:
                wt = eliminate(wt)
        w[t] = out
        if last:
            break
        solved = jnp.concatenate([xt, wt], 1)
        g = t + 1
        m = [lane_b(x[g], 8 * t + j) for j in range(8)]
        c = [
            lane_b(x[g], 8 * g + q) - tree([m[j] * sub_b(ahead[q], j) for j in range(8)])
            for q in range(8)
        ]
        x[g] = x[g] - tree([m[j] * sub_b(xt, j) for j in range(8)])
        w[g] = w[g] - tree([m[j] * sub_b(wt, j) for j in range(8)])
    return jnp.concatenate(w, 0)


def factor_kernel(panel_ref, high_ref, low_ref, x_ref):
    blocks = PANEL // 128
    panel = panel_ref[...].reshape(PANEL, D)
    panel_row = sq_row(panel)
    panel_col = sq_col(panel)
    for i in range(blocks):
        s = slice(i * 128, i * 128 + 128)
        block = gram(panel[s], panel, panel_col[s], panel_row)
        eye = iota((128, PANEL), 1) == iota((128, PANEL), 0) + i * 128
        x_ref[s, :] = block + jnp.where(eye, RIDGE, 0.0)
    sub = iota((8, 128), 0)

    def step(k, _):
        k0 = pl.multiple_of(k * 128, 128)
        at_k = pl.ds(k0, 128)
        diag = x_ref[at_k, at_k]
        inverse = inverse_factor_128([diag[8 * g : 8 * g + 8] for g in range(16)], sub)
        x_ref[at_k, at_k] = jnp.where(iota((128, 128), 0) == iota((128, 128), 1), 1.0, 0.0)
        strip = dot3(split(inverse), split(x_ref[at_k, :]), NN)
        x_ref[at_k, :] = strip
        strip = split(strip)

        def update(i, _):
            at_i = pl.ds(pl.multiple_of(i * 128, 128), 128)
            left = split(x_ref[at_k, at_i])
            x_ref[at_i, at_k] = jnp.zeros((128, 128), F32)
            x_ref[at_i, :] -= dot3(left, strip, TN)
            return 0

        lax.fori_loop(k + 1, blocks, update, 0)
        return 0

    lax.fori_loop(0, blocks, step, 0)
    for i in range(blocks):
        s = slice(i * 128, i * 128 + 128)
        lower = iota((128, PANEL), 1) < (i + 1) * 128
        high, low = split(jnp.where(lower, x_ref[s, :], 0.0))
        high_ref[s, :] = high
        low_ref[s, :] = low


COL_TILE = 256
ROW_TILE = 512
BLOCK = 256


def tile_kernel(
    where_ref, both_ref, col_ref, high_ref, low_ref, schur_ref, factor_ref,
    gh_ref, gl_ref, zh_ref, zl_ref, row_sq_ref, panel_sq_ref
):
    my_row, my_col, owner = where_ref[0], where_ref[1], where_ref[2]
    panel = both_ref[:, 1].reshape(PANEL, D)
    step = pl.program_id(0)

    @pl.when(step == 0)
    def _():
        panel_sq_ref[...] = jnp.broadcast_to(sq_row(panel), (8, PANEL))

        def rows_part(h, _):
            h0 = pl.multiple_of(h * ROW_TILE, ROW_TILE)
            at = pl.ds(h0, ROW_TILE)
            per = ROW_TILE // GROUP
            rows = both_ref[pl.ds(h * per, per), 0].reshape(ROW_TILE, D)
            rows_sq = sq_col(rows)
            row_sq_ref[at, :] = rows_sq
            ridge = jnp.where(my_row == owner, RIDGE, 0.0)
            shape = (ROW_TILE, BLOCK)
            for b in range(PANEL // BLOCK):
                s = slice(b * BLOCK, (b + 1) * BLOCK)
                block = gram(rows, panel[s], rows_sq, panel_sq_ref[0:1, s])
                eye = iota(shape, 1) + b * BLOCK == iota(shape, 0) + h0
                block = block + jnp.where(eye, ridge, 0.0)
                gh_ref[at, s], gl_ref[at, s] = split(block)
            share = jnp.zeros((ROW_TILE, GROUP), F32)
            for b in range(PANEL // BLOCK):
                s, upto = slice(b * BLOCK, (b + 1) * BLOCK), slice(0, (b + 1) * BLOCK)
                factor = dot3(
                    (gh_ref[at, upto], gl_ref[at, upto]),
                    (high_ref[s, upto], low_ref[s, upto]),
                    NT,
                )
                zh_ref[at, s], zl_ref[at, s] = split(factor)
                share = jnp.where(my_col == 2 * b, factor[:, :GROUP], share)
                share = jnp.where(my_col == 2 * b + 1, factor[:, GROUP:], share)
            factor_ref[at, :] = share
            for b in range(PANEL // BLOCK):
                s, upon = slice(b * BLOCK, (b + 1) * BLOCK), slice(b * BLOCK, PANEL)
                zh_ref[at, s], zl_ref[at, s] = split(
                    dot3(
                        (zh_ref[at, upon], zl_ref[at, upon]),
                        (high_ref[upon, s], low_ref[upon, s]),
                        NN,
                    )
                )
            return 0

        lax.fori_loop(0, PANEL // ROW_TILE, rows_part, 0)

    cols = col_ref[...]
    block = split(gram(cols, panel, sq_col(cols), panel_sq_ref[0:1, :]))
    cols_sq = sq_row(cols)
    for h in range(PANEL // ROW_TILE):
        s = slice(h * ROW_TILE, (h + 1) * ROW_TILE)
        per = ROW_TILE // GROUP
        rows = both_ref[h * per : (h + 1) * per, 0].reshape(ROW_TILE, D)
        tile = gram(rows, cols, row_sq_ref[s, :], cols_sq)
        schur_ref[s, :] = tile - dot3((zh_ref[s, :], zl_ref[s, :]), block, NT)

    @pl.when(step == owner // 2)
    def _():
        at = pl.ds(pl.multiple_of((owner % 2) * GROUP, GROUP), GROUP)
        of = pl.ds(pl.multiple_of(my_col * GROUP, GROUP), GROUP)
        z = zh_ref[:, of].astype(F32) + zl_ref[:, of].astype(F32)
        schur_ref[:, at] = schur_ref[:, at] - RIDGE * z

    @pl.when(step == my_row // 2)
    def _():
        at = pl.ds(pl.multiple_of((my_row % 2) * GROUP, GROUP), GROUP)
        of = pl.ds(pl.multiple_of(my_col * GROUP, GROUP), GROUP)
        eye = iota((GROUP, GROUP), 0) == iota((GROUP, GROUP), 1)
        schur_ref[of, at] = schur_ref[of, at] + jnp.where(eye, RIDGE, 0.0)


VMEM = pl.BlockSpec(memory_space=pltpu.VMEM)
SMEM = pl.BlockSpec(memory_space=pltpu.SMEM)


def call(kernel, out_shape, in_specs, scratch=(), **more):
    return pl.pallas_call(
        kernel,
        out_shape=out_shape,
        in_specs=in_specs,
        scratch_shapes=scratch,
        compiler_params=pltpu.CompilerParams(vmem_limit_bytes=56 << 20),
        **more,
    )


def body(descriptors, center_index, panel_index):
    my_row = lax.axis_index("row")
    my_col = lax.axis_index("col")
    owner = panel_index[0]
    flat = my_row * N_COL + my_col
    where = jnp.stack([flat, owner * N_COL, my_col, my_row, owner])
    index = center_index.reshape(DEVICES, GROUP)
    sent = call(
        send_kernel, jax.ShapeDtypeStruct((DEVICES * SLOTS, D), BF), [SMEM, VMEM, VMEM]
    )(where, index, descriptors)
    arrived = lax.all_to_all(sent, ("row", "col"), 0, 0, tiled=True)
    mine, own = call(
        take_kernel,
        (jax.ShapeDtypeStruct((2, GROUP, D), BF), jax.ShapeDtypeStruct((GROUP, D), BF)),
        [SMEM, VMEM, VMEM],
    )(where, index, arrived)
    both = lax.all_gather(mine, "col", axis=0)
    cols = lax.all_gather(own, "row", axis=0, tiled=True)
    square = jax.ShapeDtypeStruct((PANEL, PANEL), BF)
    high, low = call(
        factor_kernel,
        (square, square),
        [pl.BlockSpec((N_COL, 1, GROUP, D), lambda i: (0, 1, 0, 0))],
        [pltpu.VMEM((PANEL, PANEL), F32)],
        grid=(1,),
        out_specs=(pl.BlockSpec((PANEL, PANEL), lambda i: (0, 0)),) * 2,
    )(both)
    width = N_ROW * GROUP
    half = pltpu.VMEM((PANEL, PANEL), BF)
    schur, factor = call(
        tile_kernel,
        (
            jax.ShapeDtypeStruct((PANEL, width), F32),
            jax.ShapeDtypeStruct((PANEL, GROUP), F32),
        ),
        [SMEM, VMEM, pl.BlockSpec((COL_TILE, D), lambda i: (i, 0)), VMEM, VMEM],
        [half, half, half, half, pltpu.VMEM((PANEL, 128), F32), pltpu.VMEM((8, PANEL), F32)],
        grid=(width // COL_TILE,),
        out_specs=(
            pl.BlockSpec((PANEL, COL_TILE), lambda i: (0, i)),
            pl.BlockSpec((PANEL, GROUP), lambda i: (0, 0)),
        ),
    )(jnp.stack([my_row, my_col, owner]), both, cols, high, low)
    return schur, factor


def solution(mesh):
    return jax.shard_map(
        body,
        mesh=mesh,
        in_specs=(P(("row", "col"), None), P(), P()),
        out_specs=(P("row", "col"), P("row", "col")),
        check_vma=False,
    )
```

```python
import functools

import jax
import jax.numpy as jnp
from jax import lax
from jax.experimental import pallas as pl
from jax.experimental.pallas import tpu as pltpu
from jax.sharding import PartitionSpec as P

D = 512
PANEL = 1024
GROUP = 128
DATA_DEV = 1024
CAP = 4
N_ROW = 16
N_COL = 8
DEVICES = 128
RIDGE = 1.0
SLOTS = 2 * CAP
HOPS = (0, 1, 3, 2)
BLOCK = 256
F32 = jnp.float32
BF = jnp.bfloat16
NT = (((1,), (1,)), ((), ()))
NN = (((1,), (0,)), ((), ()))
TN = (((0,), (0,)), ((), ()))


def dot(a, b, dims):
    return lax.dot_general(a, b, dims, preferred_element_type=F32)


def split(x):
    high = x.astype(BF)
    return high, (x - high.astype(F32)).astype(BF)


def dot3(a, b, dims):
    (ah, al), (bh, bl) = a, b
    return dot(ah, bh, dims) + (dot(ah, bl, dims) + dot(al, bh, dims))


def iota(shape, dim):
    return lax.broadcasted_iota(jnp.int32, shape, dim)


K_EXP = 1.4426950408889634 / D


def sq_col(x):
    x = x.astype(F32)
    return jnp.sum(x * x, axis=1, keepdims=True) * K_EXP


def as_row(col):
    square = (128, 128)
    eye = iota(square, 0) == iota(square, 1)
    parts = [
        jnp.sum(jnp.where(eye, col[i : i + 128], 0.0), axis=0, keepdims=True)
        for i in range(0, col.shape[0], 128)
    ]
    return jnp.concatenate(parts, 1)


def gram(left, right, left_sq, right_sq):
    return jnp.exp2((dot(left, right, NT) * (2.0 * K_EXP) - left_sq) - right_sq)


def widen(x):
    return jnp.concatenate([x] * (COL_TILE // 128), 1)


def store_halves(ref, cols, x):
    n = x.shape[0]
    high, low = split(x)
    ref[:n, cols] = high
    ref[n:, cols] = low


def stacked_dot(stacked, right, dims):
    n = stacked.shape[0] // 2
    high, low = right
    both = dot(stacked, high, dims)
    return both[:n] + (both[n:] + dot(stacked[:n], low, dims))


def send_kernel(where_ref, index_ref, desc_ref, out_ref):
    flat, first = where_ref[0], where_ref[1]
    square = (GROUP, GROUP)
    index = index_ref[...]
    match = lax.shift_right_logical(index, 10) == flat
    local = jnp.bitwise_and(index, DATA_DEV - 1).astype(F32)
    before = (iota(square, 0) < iota(square, 1)).astype(BF)
    rank = dot(match.astype(BF), before, NN)
    lane = iota(square, 1)
    own = jnp.zeros(square, F32)
    panel = jnp.zeros(square, F32)
    for k in range(CAP):
        slot = match & (rank == k)
        row = jnp.sum(jnp.where(slot, local, 0.0), axis=1, keepdims=True)
        own = jnp.where(lane == k, row, own)
        panel = jnp.where(lane == k + CAP, row, panel)
    pick = (lane == first + jnp.bitwise_and(iota(square, 0), N_COL - 1)).astype(BF)
    high, low = split(panel)
    high, low = split(own + (dot(pick, high, NN) + dot(pick, low, NN)))
    desc = desc_ref[...]
    step = 256
    for i in range(0, DEVICES * SLOTS, step):
        at = iota((step, DEVICES), 0) + i
        pick = (iota((step, DEVICES), 1) == lax.shift_right_logical(at, 3)).astype(BF)
        rows = dot(pick, high, NN) + dot(pick, low, NN)
        mine = iota((step, DEVICES), 1) == jnp.bitwise_and(at, SLOTS - 1)
        row = jnp.sum(jnp.where(mine, rows, 0.0), axis=1, keepdims=True)
        pick = (iota((step, DATA_DEV), 1).astype(F32) == row).astype(BF)
        out_ref[i : i + step] = dot(pick, desc, NN).astype(BF)


def take_group(index_row, arrived, base):
    square = (GROUP, GROUP)
    shard_row = lax.shift_right_logical(index_row, 10).astype(F32)
    shard_row = jnp.broadcast_to(shard_row, square)
    eye = iota(square, 0) == iota(square, 1)
    shard_col = jnp.sum(jnp.where(eye, shard_row, 0.0), axis=1, keepdims=True)
    earlier = iota(square, 1) < iota(square, 0)
    rank = jnp.sum(
        jnp.where((shard_row == shard_col) & earlier, 1.0, 0.0), axis=1, keepdims=True
    )
    at = shard_col * SLOTS + rank + base
    pick = (iota((GROUP, DEVICES * SLOTS), 1).astype(F32) == at).astype(BF)
    return dot(pick, arrived, NN).astype(BF)


def take_kernel(where_ref, index_ref, arrived_ref, both_ref, own_ref):
    flat, first, my_col = where_ref[0], where_ref[1], where_ref[2]
    arrived = arrived_ref[...]
    own = take_group(index_ref[pl.ds(flat, 1), :], arrived, 0)
    both_ref[0] = own
    own_ref[...] = own
    both_ref[1] = take_group(index_ref[pl.ds(first + my_col, 1), :], arrived, CAP)


def lane_b(x, c):
    return jnp.broadcast_to(x[:, c : c + 1], (8, 128))


def sub_b(x, j):
    return jnp.broadcast_to(x[j : j + 1, :], (8, 128))


def tree(terms):
    while len(terms) > 1:
        pairs = [terms[i] + terms[i + 1] for i in range(0, len(terms) - 1, 2)]
        terms = pairs + terms[len(terms) & ~1 :]
    return terms[0]


def far_update(x, w, solved, t):
    pad = jnp.zeros((8, 256), F32)
    rows = jnp.concatenate([solved, pad] if t % 2 == 0 else [pad, solved], 0)
    k = t // 2

    def place(part):
        above = [jnp.zeros((16 * k, 256), BF)] if k else []
        below = [jnp.zeros((112 - 16 * k, 256), BF)] if k < 7 else []
        return jnp.concatenate(above + [part] + below, 0)

    high, low = split(rows)
    far = jnp.concatenate(x[t + 2 :], 0)
    change = dot3(split(far), (place(high), place(low)), NN)
    for i, g in enumerate(range(t + 2, 16)):
        part = change[8 * i : 8 * i + 8]
        x[g] = x[g] - part[:, :128]
        w[g] = w[g] - part[:, 128:]


def inverse_factor_128(x, sub):
    lane = iota((8, 128), 1)
    w = [(lane == sub + 8 * g).astype(F32) for g in range(16)]
    c = [lane_b(x[0], j) for j in range(8)]
    solved = None
    for t in range(16):
        last = t == 15
        if 0 < t < 15:
            far_update(x, w, solved, t - 1)
        ahead = [] if last else [lane_b(x[t], 8 * t + 8 + q) for q in range(8)]
        xt, wt = x[t], w[t]
        out = wt
        for j in range(0, 8, 2):
            p, q, r = sub_b(c[j], j), sub_b(c[j + 1], j), sub_b(c[j + 1], j + 1)
            det = p * r - q * q
            over = 1.0 / det
            root = lax.rsqrt(p)
            over_p = root * root
            at0, at1 = sub == j, sub == j + 1
            m0 = jnp.where(at0, -1.0, jnp.where(at1, 0.0, c[j]))
            m1 = jnp.where(at1, -1.0, jnp.where(at0, 0.0, c[j + 1]))
            k0 = (m0 * r - m1 * q) * over
            k1 = (m1 * p - m0 * q) * over
            keep = jnp.logical_not(at0 | at1)

            def eliminate(v):
                return jnp.where(keep, v, 0.0) - (k0 * sub_b(v, j) + k1 * sub_b(v, j + 1))

            w0, w1 = sub_b(wt, j), sub_b(wt, j + 1)
            out = jnp.where(at0, w0 * root, out)
            out = jnp.where(at1, (w1 - (q * over_p) * w0) * lax.rsqrt(det * over_p), out)
            for i in range(j + 2, 8):
                c[i] = eliminate(c[i])
            if not last:
                ahead = [eliminate(v) for v in ahead]
                xt = eliminate(xt)
            if not last or j < 6:
                wt = eliminate(wt)
        w[t] = out
        if last:
            break
        solved = jnp.concatenate([xt, wt], 1)
        g = t + 1
        m = [lane_b(x[g], 8 * t + j) for j in range(8)]
        c = [
            lane_b(x[g], 8 * g + q) - tree([m[j] * sub_b(ahead[q], j) for j in range(8)])
            for q in range(8)
        ]
        x[g] = x[g] - tree([m[j] * sub_b(xt, j) for j in range(8)])
        w[g] = w[g] - tree([m[j] * sub_b(wt, j) for j in range(8)])
    return jnp.concatenate(w, 0)


def place(blocks_ref, k, first, out_ref):
    for i, hop in enumerate(HOPS):
        at = jnp.bitwise_and(first // 2 - hop, 3) * 2 + jnp.bitwise_and(first, 1)
        out_ref[pl.ds(pl.multiple_of(at * GROUP, GROUP), GROUP), :] = blocks_ref[i, k]


def factor_kernel(where_ref, mine_ref, other_ref, high_ref, low_ref, x_ref, panel_ref):
    blocks = PANEL // 128
    my_col = where_ref[2]
    place(mine_ref, 0, my_col, panel_ref)
    place(other_ref, 0, my_col + 1 - 2 * jnp.bitwise_and(my_col, 1), panel_ref)
    panel = panel_ref[...]
    panel_col = sq_col(panel)
    panel_row = as_row(panel_col)
    for i in range(0, PANEL, BLOCK):
        s = slice(i, i + BLOCK)
        x_ref[:, s] = gram(panel, panel[s], panel_col, panel_row[:, s])
        eye = iota((BLOCK, BLOCK), 1) == iota((BLOCK, BLOCK), 0)
        x_ref[s, s] = x_ref[s, s] + jnp.where(eye, RIDGE, 0.0)
    sub = iota((8, 128), 0)

    def step(k, _):
        k0 = pl.multiple_of(k * 128, 128)
        at_k = pl.ds(k0, 128)
        diag = x_ref[at_k, at_k]
        inverse = inverse_factor_128([diag[8 * g : 8 * g + 8] for g in range(16)], sub)
        x_ref[at_k, at_k] = jnp.where(iota((128, 128), 0) == iota((128, 128), 1), 1.0, 0.0)
        strip = dot3(split(inverse), split(x_ref[at_k, :]), NN)
        x_ref[at_k, :] = strip
        strip = split(strip)

        def update(i, _):
            at_i = pl.ds(pl.multiple_of(i * 128, 128), 128)
            left = split(x_ref[at_k, at_i])
            x_ref[at_i, at_k] = jnp.zeros((128, 128), F32)
            x_ref[at_i, :] -= dot3(left, strip, TN)
            return 0

        lax.fori_loop(k + 1, blocks, update, 0)
        return 0

    lax.fori_loop(0, blocks, step, 0)
    for i in range(blocks):
        s = slice(i * 128, i * 128 + 128)
        lower = iota((128, PANEL), 1) < (i + 1) * 128
        high, low = split(jnp.where(lower, x_ref[s, :], 0.0))
        high_ref[s, :] = high
        low_ref[s, :] = low


COL_TILE = 256


def tile_kernel(
    where_ref, mine_ref, other_ref, c0_ref, c1_ref, c2_ref, c3_ref, high_ref, low_ref,
    schur_ref, factor_ref,
    g_ref, z_ref, row_sq_ref, panel_sq_ref, rows_ref, panel_ref, cols_ref
):
    my_col, my_row, owner = where_ref[2], where_ref[3], where_ref[4]
    step = pl.program_id(0)

    @pl.when(step == 0)
    def _():
        other = my_col + 1 - 2 * jnp.bitwise_and(my_col, 1)
        place(mine_ref, 0, my_col, rows_ref)
        place(other_ref, 0, other, rows_ref)
        place(mine_ref, 1, my_col, panel_ref)
        place(other_ref, 1, other, panel_ref)
        for i, c_ref in enumerate((c0_ref, c1_ref, c2_ref, c3_ref)):
            y = jnp.bitwise_and(my_row // 4 - HOPS[i], 3)
            for k, hop in enumerate(HOPS):
                r = y * 4 + jnp.bitwise_and(my_row - hop, 3)
                at = pl.ds(pl.multiple_of(r * GROUP, GROUP), GROUP)
                cols_ref[at, :] = c_ref[k * GROUP : (k + 1) * GROUP, :]
        rows, panel = rows_ref[...], panel_ref[...]
        rows_sq, panel_sq = sq_col(rows), sq_col(panel)
        row_sq_ref[...] = jnp.broadcast_to(rows_sq, (PANEL, 128))
        panel_sq_ref[...] = jnp.broadcast_to(panel_sq, (PANEL, 128))
        panel_row = as_row(panel_sq)
        ridge = jnp.where(my_row == owner, RIDGE, 0.0)
        for b in range(0, PANEL, BLOCK):
            s = slice(b, b + BLOCK)
            block = gram(rows, panel[s], rows_sq, panel_row[:, s])
            eye = iota((PANEL, BLOCK), 1) + b == iota((PANEL, BLOCK), 0)
            store_halves(g_ref, s, block + jnp.where(eye, ridge, 0.0))
        share = jnp.zeros((PANEL, GROUP), F32)
        for b in range(0, PANEL, BLOCK):
            s, upto = slice(b, b + BLOCK), slice(0, b + BLOCK)
            factor = stacked_dot(g_ref[:, upto], (high_ref[s, upto], low_ref[s, upto]), NT)
            store_halves(z_ref, s, factor)
            share = jnp.where(my_col == b // GROUP, factor[:, :GROUP], share)
            share = jnp.where(my_col == b // GROUP + 1, factor[:, GROUP:], share)
        factor_ref[...] = share
        for b in range(0, PANEL, BLOCK):
            s, upon = slice(b, b + BLOCK), slice(b, PANEL)
            z = stacked_dot(z_ref[:, upon], (high_ref[upon, s], low_ref[upon, s]), NN)
            store_halves(z_ref, s, z)

    cols = cols_ref[pl.ds(pl.multiple_of(step * COL_TILE, COL_TILE), COL_TILE), :]
    cols_sq = as_row(sq_col(cols))
    block = split(gram(panel_ref[...], cols, widen(panel_sq_ref[...]), cols_sq))
    tile = gram(rows_ref[...], cols, widen(row_sq_ref[...]), cols_sq)
    schur_ref[...] = tile - stacked_dot(z_ref[...], block, NN)

    @pl.when(step == owner // 2)
    def _():
        at = pl.ds(pl.multiple_of((owner % 2) * GROUP, GROUP), GROUP)
        of = pl.ds(pl.multiple_of(my_col * GROUP, GROUP), GROUP)
        z = z_ref[:PANEL, of].astype(F32) + z_ref[PANEL:, of].astype(F32)
        schur_ref[:, at] = schur_ref[:, at] - RIDGE * z

    @pl.when(step == my_row // 2)
    def _():
        at = pl.ds(pl.multiple_of((my_row % 2) * GROUP, GROUP), GROUP)
        of = pl.ds(pl.multiple_of(my_col * GROUP, GROUP), GROUP)
        eye = iota((GROUP, GROUP), 0) == iota((GROUP, GROUP), 1)
        schur_ref[of, at] = schur_ref[of, at] + jnp.where(eye, RIDGE, 0.0)


VMEM = pl.BlockSpec(memory_space=pltpu.VMEM)
SMEM = pl.BlockSpec(memory_space=pltpu.SMEM)


def call(kernel, out_shape, in_specs, scratch=(), **more):
    return pl.pallas_call(
        kernel,
        out_shape=out_shape,
        in_specs=in_specs,
        scratch_shapes=scratch,
        compiler_params=pltpu.CompilerParams(vmem_limit_bytes=40 << 20),
        **more,
    )


def body(descriptors, center_index, panel_index):
    my_row = lax.axis_index("row")
    my_col = lax.axis_index("col")
    owner = panel_index[0]
    flat = my_row * N_COL + my_col
    where = jnp.stack([flat, owner * N_COL, my_col, my_row, owner])
    index = center_index.reshape(DEVICES, GROUP)
    sent = call(
        send_kernel, jax.ShapeDtypeStruct((DEVICES * SLOTS, D), BF), [SMEM, VMEM, VMEM]
    )(where, index, descriptors)
    arrived = lax.all_to_all(sent, ("row", "col"), 0, 0, tiled=True)
    mine, own = call(
        take_kernel,
        (jax.ShapeDtypeStruct((2, GROUP, D), BF), jax.ShapeDtypeStruct((GROUP, D), BF)),
        [SMEM, VMEM, VMEM],
    )(where, index, arrived)
    near = [mine] + [
        lax.ppermute(mine, "col", [(i, (i // 2 + h) % 4 * 2 + i % 2) for i in range(N_COL)])
        for h in HOPS[1:]
    ]
    cols = [own] + [
        lax.ppermute(own, "row", [(i, i // 4 * 4 + (i + h) % 4) for i in range(N_ROW)])
        for h in HOPS[1:]
    ]
    near, cols = lax.optimization_barrier((near, cols))
    near = jnp.stack(near)
    cols = jnp.concatenate(cols, 0)
    other = lax.ppermute(near, "col", [(i, i ^ 1) for i in range(N_COL)])
    cols = [cols] + [
        lax.ppermute(cols, "row", [(i, (i // 4 + h) % 4 * 4 + i % 4) for i in range(N_ROW)])
        for h in HOPS[1:]
    ]
    square = jax.ShapeDtypeStruct((PANEL, PANEL), BF)
    pieces = pl.BlockSpec((4, 1, GROUP, D), lambda i: (0, 1, 0, 0))
    high, low = call(
        factor_kernel,
        (square, square),
        [SMEM, pieces, pieces],
        [pltpu.VMEM((PANEL, PANEL), F32), pltpu.VMEM((PANEL, D), BF)],
        grid=(1,),
        out_specs=(pl.BlockSpec((PANEL, PANEL), lambda i: (0, 0)),) * 2,
    )(where, near, other)
    width = N_ROW * GROUP
    halves = pltpu.VMEM((2 * PANEL, PANEL), BF)
    squares = pltpu.VMEM((PANEL, 128), F32)
    schur, factor = call(
        tile_kernel,
        (
            jax.ShapeDtypeStruct((PANEL, width), F32),
            jax.ShapeDtypeStruct((PANEL, GROUP), F32),
        ),
        [SMEM] + [VMEM] * 8,
        [halves, halves, squares, squares]
        + [pltpu.VMEM((PANEL, D), BF), pltpu.VMEM((PANEL, D), BF), pltpu.VMEM((width, D), BF)],
        grid=(width // COL_TILE,),
        out_specs=(
            pl.BlockSpec((PANEL, COL_TILE), lambda i: (0, i)),
            pl.BlockSpec((PANEL, GROUP), lambda i: (0, 0)),
        ),
    )(where, near, other, *cols, high, low)
    return schur, factor


def solution(mesh):
    return jax.shard_map(
        body,
        mesh=mesh,
        in_specs=(P(("row", "col"), None), P(), P()),
        out_specs=(P("row", "col"), P("row", "col")),
        check_vma=False,
    )
```

```python
import functools

import jax
import jax.numpy as jnp
from jax import lax
from jax.experimental import pallas as pl
from jax.experimental.pallas import tpu as pltpu
from jax.sharding import PartitionSpec as P

D = 512
PANEL = 1024
GROUP = 128
DATA_DEV = 1024
CAP = 4
N_ROW = 16
N_COL = 8
DEVICES = 128
RIDGE = 1.0
SLOTS = 2 * CAP
HOPS = (0, 1, 3, 2)
BLOCK = 256
UNROLLED = 4
F32 = jnp.float32
BF = jnp.bfloat16
NT = (((1,), (1,)), ((), ()))
NN = (((1,), (0,)), ((), ()))
TN = (((0,), (0,)), ((), ()))


def dot(a, b, dims):
    return lax.dot_general(a, b, dims, preferred_element_type=F32)


def split(x):
    high = x.astype(BF)
    return high, (x - high.astype(F32)).astype(BF)


def by_left(halves):
    high, low = halves
    return jnp.concatenate([high, low, high], 1)


def by_top(halves):
    high, low = halves
    return jnp.concatenate([high, low, high], 0)


def by_right(halves):
    high, low = halves
    return jnp.concatenate([high, high, low], 0)


def iota(shape, dim):
    return lax.broadcasted_iota(jnp.int32, shape, dim)


K_EXP = 1.4426950408889634 / D


def sq_col(x):
    x = x.astype(F32)
    return jnp.sum(x * x, axis=1, keepdims=True) * K_EXP


def as_row(col):
    square = (128, 128)
    eye = iota(square, 0) == iota(square, 1)
    parts = [
        jnp.sum(jnp.where(eye, col[i : i + 128], 0.0), axis=0, keepdims=True)
        for i in range(0, col.shape[0], 128)
    ]
    return jnp.concatenate(parts, 1)


def gram(left, right, left_sq, right_sq):
    return jnp.exp2((dot(left, right, NT) * (2.0 * K_EXP) - left_sq) - right_sq)


def widen(x):
    return jnp.concatenate([x] * (COL_TILE // 128), 1)


def store_halves(ref, cols, x):
    n = x.shape[0]
    high, low = split(x)
    ref[:n, cols] = high
    ref[n:, cols] = low


def stacked_dot(stacked, right, dims):
    n = stacked.shape[0] // 2
    high, low = right
    both = dot(stacked, high, dims)
    return both[:n] + (both[n:] + dot(stacked[:n], low, dims))


def send_kernel(where_ref, index_ref, desc_ref, out_ref):
    flat, first = where_ref[0], where_ref[1]
    square = (GROUP, GROUP)
    index = index_ref[...]
    match = lax.shift_right_logical(index, 10) == flat
    local = jnp.bitwise_and(index, DATA_DEV - 1).astype(F32)
    before = (iota(square, 0) < iota(square, 1)).astype(BF)
    rank = dot(match.astype(BF), before, NN)
    lane = iota(square, 1)
    own = jnp.zeros(square, F32)
    panel = jnp.zeros(square, F32)
    for k in range(CAP):
        slot = match & (rank == k)
        row = jnp.sum(jnp.where(slot, local, 0.0), axis=1, keepdims=True)
        own = jnp.where(lane == k, row, own)
        panel = jnp.where(lane == k + CAP, row, panel)
    pick = (lane == first + jnp.bitwise_and(iota(square, 0), N_COL - 1)).astype(BF)
    high, low = split(panel)
    high, low = split(own + (dot(pick, high, NN) + dot(pick, low, NN)))
    desc = desc_ref[...]
    step = 256
    for i in range(0, DEVICES * SLOTS, step):
        at = iota((step, DEVICES), 0) + i
        pick = (iota((step, DEVICES), 1) == lax.shift_right_logical(at, 3)).astype(BF)
        rows = dot(pick, high, NN) + dot(pick, low, NN)
        mine = iota((step, DEVICES), 1) == jnp.bitwise_and(at, SLOTS - 1)
        row = jnp.sum(jnp.where(mine, rows, 0.0), axis=1, keepdims=True)
        pick = (iota((step, DATA_DEV), 1).astype(F32) == row).astype(BF)
        out_ref[i : i + step] = dot(pick, desc, NN).astype(BF)


def take_group(index_row, arrived, base):
    square = (GROUP, GROUP)
    shard_row = lax.shift_right_logical(index_row, 10).astype(F32)
    shard_row = jnp.broadcast_to(shard_row, square)
    eye = iota(square, 0) == iota(square, 1)
    shard_col = jnp.sum(jnp.where(eye, shard_row, 0.0), axis=1, keepdims=True)
    earlier = iota(square, 1) < iota(square, 0)
    rank = jnp.sum(
        jnp.where((shard_row == shard_col) & earlier, 1.0, 0.0), axis=1, keepdims=True
    )
    at = shard_col * SLOTS + rank + base
    pick = (iota((GROUP, DEVICES * SLOTS), 1).astype(F32) == at).astype(BF)
    return dot(pick, arrived, NN).astype(BF)


def take_kernel(where_ref, index_ref, arrived_ref, both_ref, own_ref):
    flat, first, my_col = where_ref[0], where_ref[1], where_ref[2]
    arrived = arrived_ref[...]
    own = take_group(index_ref[pl.ds(flat, 1), :], arrived, 0)
    both_ref[0] = own
    own_ref[...] = own
    both_ref[1] = take_group(index_ref[pl.ds(first + my_col, 1), :], arrived, CAP)


def lane_b(x, c):
    return jnp.broadcast_to(x[:, c : c + 1], (8, 128))


def sub_b(x, j):
    return jnp.broadcast_to(x[j : j + 1, :], (8, 128))


def tree(terms):
    while len(terms) > 1:
        pairs = [terms[i] + terms[i + 1] for i in range(0, len(terms) - 1, 2)]
        terms = pairs + terms[len(terms) & ~1 :]
    return terms[0]


def far_update(x, w, solved, t):
    pad = jnp.zeros((8, 256), F32)
    rows = jnp.concatenate([solved, pad] if t % 2 == 0 else [pad, solved], 0)
    k = t // 2

    def place(part):
        above = [jnp.zeros((16 * k, 256), BF)] if k else []
        below = [jnp.zeros((112 - 16 * k, 256), BF)] if k < 7 else []
        return jnp.concatenate(above + [part] + below, 0)

    high, low = map(place, split(rows))
    far = jnp.concatenate(x[t + 2 :], 0)
    right = jnp.concatenate(
        [
            jnp.concatenate([high, low], 1),
            jnp.concatenate([high, jnp.zeros((128, 256), BF)], 1),
        ],
        0,
    )
    change = dot(jnp.concatenate(split(far), 1), right, NN)
    change = change[:, :256] + change[:, 256:]
    for i, g in enumerate(range(t + 2, 16)):
        part = change[8 * i : 8 * i + 8]
        x[g] = x[g] - part[:, :128]
        w[g] = w[g] - part[:, 128:]


def inverse_factor_128(x, sub):
    lane = iota((8, 128), 1)
    w = [(lane == sub + 8 * g).astype(F32) for g in range(16)]
    c = [lane_b(x[0], j) for j in range(8)]
    solved = None
    for t in range(16):
        last = t == 15
        if 0 < t < 15:
            far_update(x, w, solved, t - 1)
        ahead = [] if last else [lane_b(x[t], 8 * t + 8 + q) for q in range(8)]
        xt, wt = x[t], w[t]
        out = wt
        for j in range(0, 8, 2):
            p, q, r = sub_b(c[j], j), sub_b(c[j + 1], j), sub_b(c[j + 1], j + 1)
            det = p * r - q * q
            over = 1.0 / det
            root = lax.rsqrt(p)
            over_p = root * root
            at0, at1 = sub == j, sub == j + 1
            m0 = jnp.where(at0, -1.0, jnp.where(at1, 0.0, c[j]))
            m1 = jnp.where(at1, -1.0, jnp.where(at0, 0.0, c[j + 1]))
            k0 = (m0 * r - m1 * q) * over
            k1 = (m1 * p - m0 * q) * over
            keep = jnp.logical_not(at0 | at1)

            def eliminate(v):
                return jnp.where(keep, v, 0.0) - (k0 * sub_b(v, j) + k1 * sub_b(v, j + 1))

            w0, w1 = sub_b(wt, j), sub_b(wt, j + 1)
            out = jnp.where(at0, w0 * root, out)
            out = jnp.where(at1, (w1 - (q * over_p) * w0) * lax.rsqrt(det * over_p), out)
            for i in range(j + 2, 8):
                c[i] = eliminate(c[i])
            if not last:
                ahead = [eliminate(v) for v in ahead]
                xt = eliminate(xt)
            if not last or j < 6:
                wt = eliminate(wt)
        w[t] = out
        if last:
            break
        solved = jnp.concatenate([xt, wt], 1)
        g = t + 1
        m = [lane_b(x[g], 8 * t + j) for j in range(8)]
        c = [
            lane_b(x[g], 8 * g + q) - tree([m[j] * sub_b(ahead[q], j) for j in range(8)])
            for q in range(8)
        ]
        x[g] = x[g] - tree([m[j] * sub_b(xt, j) for j in range(8)])
        w[g] = w[g] - tree([m[j] * sub_b(wt, j) for j in range(8)])
    return jnp.concatenate(w, 0)


def place(blocks_ref, k, first, out_ref):
    for i, hop in enumerate(HOPS):
        at = jnp.bitwise_and(first // 2 - hop, 3) * 2 + jnp.bitwise_and(first, 1)
        out_ref[pl.ds(pl.multiple_of(at * GROUP, GROUP), GROUP), :] = blocks_ref[i, k]


def factor_kernel(where_ref, mine_ref, other_ref, high_ref, low_ref, x_ref, panel_ref):
    blocks = PANEL // 128
    my_col = where_ref[2]
    place(mine_ref, 0, my_col, panel_ref)
    place(other_ref, 0, my_col + 1 - 2 * jnp.bitwise_and(my_col, 1), panel_ref)
    panel = panel_ref[...]
    panel_col = sq_col(panel)
    panel_row = as_row(panel_col)
    for i in range(0, PANEL, BLOCK):
        s = slice(i, i + BLOCK)
        x_ref[:, s] = gram(panel, panel[s], panel_col, panel_row[:, s])
        eye = iota((BLOCK, BLOCK), 1) == iota((BLOCK, BLOCK), 0)
        x_ref[s, s] = x_ref[s, s] + jnp.where(eye, RIDGE, 0.0)
    sub = iota((8, 128), 0)

    def inverse_of(block):
        return inverse_factor_128([block[8 * g : 8 * g + 8] for g in range(16)], sub)

    block, pending = x_ref[0:128, 0:128], None
    for k in range(UNROLLED):
        at, after = slice(k * 128, k * 128 + 128), slice(k * 128 + 128, PANEL)
        if pending is not None:
            pending()
        inverse = inverse_of(block)
        halves = split(inverse)
        left = by_left(halves)

        def strip(cols):
            part = dot(left, by_right(split(x_ref[at, cols])), NN)
            x_ref[at, cols] = part
            return split(part)

        x_ref[at, at] = inverse
        ahead = strip(after)
        behind = strip(slice(0, k * 128)) if k else None
        top, right = by_top(ahead), by_right(ahead)
        near = slice(k * 128 + 128, k * 128 + 256)
        block = x_ref[near, near] - dot(top[:, :128], right[:, :128], TN)

        def update(k=k, at=at, after=after, halves=halves, behind=behind, top=top, right=right):
            x_ref[after, after] -= dot(top, right, TN)
            if k:
                halves = tuple(jnp.concatenate([u, v], 1) for u, v in zip(behind, halves))
            change = dot(top, by_right(halves), TN)
            if k:
                x_ref[after, : k * 128] -= change[:, : k * 128]
            x_ref[after, at] = -change[:, k * 128 :]

        pending = update
    pending()

    def step(k, _):
        k0 = pl.multiple_of(k * 128, 128)
        at_k = pl.ds(k0, 128)
        inverse = inverse_of(x_ref[at_k, at_k])
        x_ref[at_k, at_k] = jnp.where(iota((128, 128), 0) == iota((128, 128), 1), 1.0, 0.0)
        part = dot(by_left(split(inverse)), by_right(split(x_ref[at_k, :])), NN)
        x_ref[at_k, :] = part
        right = by_right(split(part))

        def update(i, _):
            at_i = pl.ds(pl.multiple_of(i * 128, 128), 128)
            top = by_top(split(x_ref[at_k, at_i]))
            x_ref[at_i, at_k] = jnp.zeros((128, 128), F32)
            x_ref[at_i, :] -= dot(top, right, TN)
            return 0

        lax.fori_loop(k + 1, blocks, update, 0)
        return 0

    lax.fori_loop(UNROLLED, blocks, step, 0)
    for i in range(blocks):
        s = slice(i * 128, i * 128 + 128)
        lower = iota((128, PANEL), 1) < (i + 1) * 128
        high, low = split(jnp.where(lower, x_ref[s, :], 0.0))
        high_ref[s, :] = high
        low_ref[s, :] = low


COL_TILE = 256


def tile_kernel(
    where_ref, mine_ref, other_ref, c0_ref, c1_ref, c2_ref, c3_ref, high_ref, low_ref,
    schur_ref, factor_ref,
    g_ref, z_ref, row_sq_ref, panel_sq_ref, rows_ref, panel_ref, cols_ref
):
    my_col, my_row, owner = where_ref[2], where_ref[3], where_ref[4]
    step = pl.program_id(0)

    @pl.when(step == 0)
    def _():
        other = my_col + 1 - 2 * jnp.bitwise_and(my_col, 1)
        place(mine_ref, 0, my_col, rows_ref)
        place(other_ref, 0, other, rows_ref)
        place(mine_ref, 1, my_col, panel_ref)
        place(other_ref, 1, other, panel_ref)
        for i, c_ref in enumerate((c0_ref, c1_ref, c2_ref, c3_ref)):
            y = jnp.bitwise_and(my_row // 4 - HOPS[i], 3)
            for k, hop in enumerate(HOPS):
                r = y * 4 + jnp.bitwise_and(my_row - hop, 3)
                at = pl.ds(pl.multiple_of(r * GROUP, GROUP), GROUP)
                cols_ref[at, :] = c_ref[k * GROUP : (k + 1) * GROUP, :]
        rows, panel = rows_ref[...], panel_ref[...]
        rows_sq, panel_sq = sq_col(rows), sq_col(panel)
        row_sq_ref[...] = jnp.broadcast_to(rows_sq, (PANEL, 128))
        panel_sq_ref[...] = jnp.broadcast_to(panel_sq, (PANEL, 128))
        panel_row = as_row(panel_sq)
        ridge = jnp.where(my_row == owner, RIDGE, 0.0)
        for b in range(0, PANEL, BLOCK):
            s = slice(b, b + BLOCK)
            block = gram(rows, panel[s], rows_sq, panel_row[:, s])
            eye = iota((PANEL, BLOCK), 1) + b == iota((PANEL, BLOCK), 0)
            store_halves(g_ref, s, block + jnp.where(eye, ridge, 0.0))
        share = jnp.zeros((PANEL, GROUP), F32)
        for b in range(0, PANEL, BLOCK):
            s, upto = slice(b, b + BLOCK), slice(0, b + BLOCK)
            factor = stacked_dot(g_ref[:, upto], (high_ref[s, upto], low_ref[s, upto]), NT)
            store_halves(z_ref, s, factor)
            share = jnp.where(my_col == b // GROUP, factor[:, :GROUP], share)
            share = jnp.where(my_col == b // GROUP + 1, factor[:, GROUP:], share)
        factor_ref[...] = share
        for b in range(0, PANEL, BLOCK):
            s, upon = slice(b, b + BLOCK), slice(b, PANEL)
            z = stacked_dot(z_ref[:, upon], (high_ref[upon, s], low_ref[upon, s]), NN)
            store_halves(z_ref, s, z)

    cols = cols_ref[pl.ds(pl.multiple_of(step * COL_TILE, COL_TILE), COL_TILE), :]
    cols_sq = as_row(sq_col(cols))
    block = split(gram(panel_ref[...], cols, widen(panel_sq_ref[...]), cols_sq))
    tile = gram(rows_ref[...], cols, widen(row_sq_ref[...]), cols_sq)
    schur_ref[...] = tile - stacked_dot(z_ref[...], block, NN)

    @pl.when(step == owner // 2)
    def _():
        at = pl.ds(pl.multiple_of((owner % 2) * GROUP, GROUP), GROUP)
        of = pl.ds(pl.multiple_of(my_col * GROUP, GROUP), GROUP)
        z = z_ref[:PANEL, of].astype(F32) + z_ref[PANEL:, of].astype(F32)
        schur_ref[:, at] = schur_ref[:, at] - RIDGE * z

    @pl.when(step == my_row // 2)
    def _():
        at = pl.ds(pl.multiple_of((my_row % 2) * GROUP, GROUP), GROUP)
        of = pl.ds(pl.multiple_of(my_col * GROUP, GROUP), GROUP)
        eye = iota((GROUP, GROUP), 0) == iota((GROUP, GROUP), 1)
        schur_ref[of, at] = schur_ref[of, at] + jnp.where(eye, RIDGE, 0.0)


VMEM = pl.BlockSpec(memory_space=pltpu.VMEM)
SMEM = pl.BlockSpec(memory_space=pltpu.SMEM)


def call(kernel, out_shape, in_specs, scratch=(), **more):
    return pl.pallas_call(
        kernel,
        out_shape=out_shape,
        in_specs=in_specs,
        scratch_shapes=scratch,
        compiler_params=pltpu.CompilerParams(vmem_limit_bytes=40 << 20),
        **more,
    )


def body(descriptors, center_index, panel_index):
    my_row = lax.axis_index("row")
    my_col = lax.axis_index("col")
    owner = panel_index[0]
    flat = my_row * N_COL + my_col
    where = jnp.stack([flat, owner * N_COL, my_col, my_row, owner])
    index = center_index.reshape(DEVICES, GROUP)
    sent = call(
        send_kernel,
        jax.ShapeDtypeStruct((DEVICES * SLOTS, D), BF),
        [SMEM, VMEM, VMEM],
    )(where, index, descriptors)
    arrived = lax.all_to_all(sent, ("row", "col"), 0, 0, tiled=True)
    mine, own = call(
        take_kernel,
        (jax.ShapeDtypeStruct((2, GROUP, D), BF), jax.ShapeDtypeStruct((GROUP, D), BF)),
        [SMEM, VMEM, VMEM],
    )(where, index, arrived)
    near = [mine] + [
        lax.ppermute(mine, "col", [(i, (i // 2 + h) % 4 * 2 + i % 2) for i in range(N_COL)])
        for h in HOPS[1:]
    ]
    cols = [own] + [
        lax.ppermute(own, "row", [(i, i // 4 * 4 + (i + h) % 4) for i in range(N_ROW)])
        for h in HOPS[1:]
    ]
    near, cols = lax.optimization_barrier((near, cols))
    near = jnp.stack(near)
    cols = jnp.concatenate(cols, 0)
    other = lax.ppermute(near, "col", [(i, i ^ 1) for i in range(N_COL)])
    cols = [cols] + [
        lax.ppermute(cols, "row", [(i, (i // 4 + h) % 4 * 4 + i % 4) for i in range(N_ROW)])
        for h in HOPS[1:]
    ]
    square = jax.ShapeDtypeStruct((PANEL, PANEL), BF)
    pieces = pl.BlockSpec((4, 1, GROUP, D), lambda i: (0, 1, 0, 0))
    high, low = call(
        factor_kernel,
        (square, square),
        [SMEM, pieces, pieces],
        [pltpu.VMEM((PANEL, PANEL), F32), pltpu.VMEM((PANEL, D), BF)],
        grid=(1,),
        out_specs=(pl.BlockSpec((PANEL, PANEL), lambda i: (0, 0)),) * 2,
    )(where, near, other)
    width = N_ROW * GROUP
    halves = pltpu.VMEM((2 * PANEL, PANEL), BF)
    squares = pltpu.VMEM((PANEL, 128), F32)
    schur, factor = call(
        tile_kernel,
        (
            jax.ShapeDtypeStruct((PANEL, width), F32),
            jax.ShapeDtypeStruct((PANEL, GROUP), F32),
        ),
        [SMEM] + [VMEM] * 8,
        [halves, halves, squares, squares]
        + [pltpu.VMEM((PANEL, D), BF), pltpu.VMEM((PANEL, D), BF), pltpu.VMEM((width, D), BF)],
        grid=(width // COL_TILE,),
        out_specs=(
            pl.BlockSpec((PANEL, COL_TILE), lambda i: (0, i)),
            pl.BlockSpec((PANEL, GROUP), lambda i: (0, 0)),
        ),
    )(where, near, other, *cols, high, low)
    return schur, factor


def solution(mesh):
    return jax.shard_map(
        body,
        mesh=mesh,
        in_specs=(P(("row", "col"), None), P(), P()),
        out_specs=(P("row", "col"), P("row", "col")),
        check_vma=False,
    )
```

```python
import functools

import jax
import jax.numpy as jnp
from jax import lax
from jax.experimental import pallas as pl
from jax.experimental.pallas import tpu as pltpu
from jax.sharding import PartitionSpec as P

D = 512
PANEL = 1024
GROUP = 128
DATA_DEV = 1024
CAP = 4
N_ROW = 16
N_COL = 8
DEVICES = 128
RIDGE = 1.0
SLOTS = 2 * CAP
HOPS = (0, 1, 3, 2)
BLOCK = 256
UNROLLED = 4
F32 = jnp.float32
BF = jnp.bfloat16
NT = (((1,), (1,)), ((), ()))
NN = (((1,), (0,)), ((), ()))
TN = (((0,), (0,)), ((), ()))


def dot(a, b, dims):
    return lax.dot_general(a, b, dims, preferred_element_type=F32)


def split(x):
    high = x.astype(BF)
    return high, (x - high.astype(F32)).astype(BF)


def by_left(halves):
    high, low = halves
    return jnp.concatenate([high, low, high], 1)


def by_top(halves):
    high, low = halves
    return jnp.concatenate([high, low, high], 0)


def by_right(halves):
    high, low = halves
    return jnp.concatenate([high, high, low], 0)


def iota(shape, dim):
    return lax.broadcasted_iota(jnp.int32, shape, dim)


K_EXP = 1.4426950408889634 / D


def sq_col(x):
    x = x.astype(F32)
    return jnp.sum(x * x, axis=1, keepdims=True) * K_EXP


def as_row(col):
    square = (128, 128)
    eye = iota(square, 0) == iota(square, 1)
    parts = [
        jnp.sum(jnp.where(eye, col[i : i + 128], 0.0), axis=0, keepdims=True)
        for i in range(0, col.shape[0], 128)
    ]
    return jnp.concatenate(parts, 1)


def gram(left, right, left_sq, right_sq):
    return jnp.exp2((dot(left, right, NT) * (2.0 * K_EXP) - left_sq) - right_sq)


def widen(x):
    return jnp.concatenate([x] * (COL_TILE // 128), 1)


def store_halves(ref, cols, x):
    n = x.shape[0]
    high, low = split(x)
    ref[:n, cols] = high
    ref[n:, cols] = low


def stacked_dot(stacked, right, dims):
    n = stacked.shape[0] // 2
    high, low = right
    both = dot(stacked, high, dims)
    return both[:n] + (both[n:] + dot(stacked[:n], low, dims))


def send_kernel(where_ref, index_ref, desc_ref, out_ref):
    flat, first = where_ref[0], where_ref[1]
    square = (GROUP, GROUP)
    index = index_ref[...]
    match = lax.shift_right_logical(index, 10) == flat
    local = jnp.bitwise_and(index, DATA_DEV - 1).astype(F32)
    before = (iota(square, 0) < iota(square, 1)).astype(BF)
    rank = dot(match.astype(BF), before, NN)
    lane = iota(square, 1)
    own = jnp.zeros(square, F32)
    panel = jnp.zeros(square, F32)
    for k in range(CAP):
        slot = match & (rank == k)
        row = jnp.sum(jnp.where(slot, local, 0.0), axis=1, keepdims=True)
        own = jnp.where(lane == k, row, own)
        panel = jnp.where(lane == k + CAP, row, panel)
    pick = (lane == first + jnp.bitwise_and(iota(square, 0), N_COL - 1)).astype(BF)
    high, low = split(panel)
    high, low = split(own + (dot(pick, high, NN) + dot(pick, low, NN)))
    desc = desc_ref[...]
    step = 256
    for i in range(0, DEVICES * SLOTS, step):
        at = iota((step, DEVICES), 0) + i
        pick = (iota((step, DEVICES), 1) == lax.shift_right_logical(at, 3)).astype(BF)
        rows = dot(pick, high, NN) + dot(pick, low, NN)
        mine = iota((step, DEVICES), 1) == jnp.bitwise_and(at, SLOTS - 1)
        row = jnp.sum(jnp.where(mine, rows, 0.0), axis=1, keepdims=True)
        pick = (iota((step, DATA_DEV), 1).astype(F32) == row).astype(BF)
        out_ref[i : i + step] = dot(pick, desc, NN).astype(BF)


def take_group(index_row, arrived, base):
    square = (GROUP, GROUP)
    shard_row = lax.shift_right_logical(index_row, 10).astype(F32)
    shard_row = jnp.broadcast_to(shard_row, square)
    eye = iota(square, 0) == iota(square, 1)
    shard_col = jnp.sum(jnp.where(eye, shard_row, 0.0), axis=1, keepdims=True)
    earlier = iota(square, 1) < iota(square, 0)
    rank = jnp.sum(
        jnp.where((shard_row == shard_col) & earlier, 1.0, 0.0), axis=1, keepdims=True
    )
    at = shard_col * SLOTS + rank + base
    pick = (iota((GROUP, DEVICES * SLOTS), 1).astype(F32) == at).astype(BF)
    return dot(pick, arrived, NN).astype(BF)


def take_kernel(where_ref, index_ref, arrived_ref, both_ref, own_ref):
    flat, first, my_col = where_ref[0], where_ref[1], where_ref[2]
    arrived = arrived_ref[...]
    own = take_group(index_ref[pl.ds(flat, 1), :], arrived, 0)
    both_ref[0] = own
    own_ref[...] = own
    both_ref[1] = take_group(index_ref[pl.ds(first + my_col, 1), :], arrived, CAP)


def lane_b(x, c):
    return jnp.broadcast_to(x[:, c : c + 1], (8, 128))


def sub_b(x, j):
    return jnp.broadcast_to(x[j : j + 1, :], (8, 128))


def tree(terms):
    while len(terms) > 1:
        pairs = [terms[i] + terms[i + 1] for i in range(0, len(terms) - 1, 2)]
        terms = pairs + terms[len(terms) & ~1 :]
    return terms[0]


def far_update(x, w, solved, t):
    pad = jnp.zeros((8, 256), F32)
    rows = jnp.concatenate([solved, pad] if t % 2 == 0 else [pad, solved], 0)
    k = t // 2

    def place(part):
        above = [jnp.zeros((16 * k, 256), BF)] if k else []
        below = [jnp.zeros((112 - 16 * k, 256), BF)] if k < 7 else []
        return jnp.concatenate(above + [part] + below, 0)

    high, low = map(place, split(rows))
    far = jnp.concatenate(x[t + 2 :], 0)
    right = jnp.concatenate(
        [
            jnp.concatenate([high, low], 1),
            jnp.concatenate([high, jnp.zeros((128, 256), BF)], 1),
        ],
        0,
    )
    change = dot(jnp.concatenate(split(far), 1), right, NN)
    change = change[:, :256] + change[:, 256:]
    for i, g in enumerate(range(t + 2, 16)):
        part = change[8 * i : 8 * i + 8]
        x[g] = x[g] - part[:, :128]
        w[g] = w[g] - part[:, 128:]


def inverse_factor_128(x, sub):
    lane = iota((8, 128), 1)
    w = [(lane == sub + 8 * g).astype(F32) for g in range(16)]
    unit = [(sub == j).astype(F32) for j in range(8)]
    c = [lane_b(x[0], j) for j in range(8)]
    solved = None
    for t in range(16):
        last = t == 15
        if 0 < t < 15:
            far_update(x, w, solved, t - 1)
        ahead = [] if last else [lane_b(x[t], 8 * t + 8 + q) for q in range(8)]
        xt, wt = x[t], w[t]
        out = wt
        for j in range(0, 8, 2):
            p, q, r = sub_b(c[j], j), sub_b(c[j + 1], j), sub_b(c[j + 1], j + 1)
            det = p * r - q * q
            over = 1.0 / det
            root = lax.rsqrt(p)
            over_p = root * root
            at0, at1 = sub == j, sub == j + 1
            m0, m1 = c[j] - unit[j], c[j + 1] - unit[j + 1]
            k0 = (m0 * r - m1 * q) * over
            k1 = (m1 * p - m0 * q) * over

            def eliminate(v):
                return v - (k0 * sub_b(v, j) + k1 * sub_b(v, j + 1))

            w0, w1 = sub_b(wt, j), sub_b(wt, j + 1)
            out = jnp.where(at0, w0 * root, out)
            out = jnp.where(at1, (w1 - (q * over_p) * w0) * lax.rsqrt(det * over_p), out)
            for i in range(j + 2, 8):
                c[i] = eliminate(c[i])
            if not last:
                ahead = [eliminate(v) for v in ahead]
                xt = eliminate(xt)
            if not last or j < 6:
                wt = eliminate(wt)
        w[t] = out
        if last:
            break
        solved = jnp.concatenate([xt, wt], 1)
        g = t + 1
        m = [lane_b(x[g], 8 * t + j) for j in range(8)]
        c = [
            lane_b(x[g], 8 * g + q) - tree([m[j] * sub_b(ahead[q], j) for j in range(8)])
            for q in range(8)
        ]
        x[g] = x[g] - tree([m[j] * sub_b(xt, j) for j in range(8)])
        w[g] = w[g] - tree([m[j] * sub_b(wt, j) for j in range(8)])
    return jnp.concatenate(w, 0)


def place(blocks_ref, k, first, out_ref):
    for i, hop in enumerate(HOPS):
        at = jnp.bitwise_and(first // 2 - hop, 3) * 2 + jnp.bitwise_and(first, 1)
        out_ref[pl.ds(pl.multiple_of(at * GROUP, GROUP), GROUP), :] = blocks_ref[i, k]


def factor_kernel(where_ref, mine_ref, other_ref, high_ref, low_ref, x_ref, panel_ref):
    blocks = PANEL // 128
    my_col = where_ref[2]
    place(mine_ref, 0, my_col, panel_ref)
    place(other_ref, 0, my_col + 1 - 2 * jnp.bitwise_and(my_col, 1), panel_ref)
    panel = panel_ref[...]
    panel_col = sq_col(panel)
    panel_row = as_row(panel_col)
    for i in range(0, PANEL, BLOCK):
        s = slice(i, i + BLOCK)
        x_ref[:, s] = gram(panel, panel[s], panel_col, panel_row[:, s])
        eye = iota((BLOCK, BLOCK), 1) == iota((BLOCK, BLOCK), 0)
        x_ref[s, s] = x_ref[s, s] + jnp.where(eye, RIDGE, 0.0)
    sub = iota((8, 128), 0)

    def inverse_of(block):
        return inverse_factor_128([block[8 * g : 8 * g + 8] for g in range(16)], sub)

    block, pending = x_ref[0:128, 0:128], None
    for k in range(UNROLLED):
        at, after = slice(k * 128, k * 128 + 128), slice(k * 128 + 128, PANEL)
        if pending is not None:
            pending()
        inverse = inverse_of(block)
        halves = split(inverse)
        left = by_left(halves)

        def strip(cols):
            part = dot(left, by_right(split(x_ref[at, cols])), NN)
            x_ref[at, cols] = part
            return split(part)

        x_ref[at, at] = inverse
        ahead = strip(after)
        behind = strip(slice(0, k * 128)) if k else None
        top, right = by_top(ahead), by_right(ahead)
        near = slice(k * 128 + 128, k * 128 + 256)
        block = x_ref[near, near] - dot(top[:, :128], right[:, :128], TN)

        def update(k=k, at=at, after=after, halves=halves, behind=behind, top=top, right=right):
            x_ref[after, after] -= dot(top, right, TN)
            if k:
                halves = tuple(jnp.concatenate([u, v], 1) for u, v in zip(behind, halves))
            change = dot(top, by_right(halves), TN)
            if k:
                x_ref[after, : k * 128] -= change[:, : k * 128]
            x_ref[after, at] = -change[:, k * 128 :]

        pending = update
    pending()

    def step(k, _):
        k0 = pl.multiple_of(k * 128, 128)
        at_k = pl.ds(k0, 128)
        inverse = inverse_of(x_ref[at_k, at_k])
        x_ref[at_k, at_k] = jnp.where(iota((128, 128), 0) == iota((128, 128), 1), 1.0, 0.0)
        part = dot(by_left(split(inverse)), by_right(split(x_ref[at_k, :])), NN)
        x_ref[at_k, :] = part
        right = by_right(split(part))

        def update(i, _):
            at_i = pl.ds(pl.multiple_of(i * 128, 128), 128)
            top = by_top(split(x_ref[at_k, at_i]))
            x_ref[at_i, at_k] = jnp.zeros((128, 128), F32)
            x_ref[at_i, :] -= dot(top, right, TN)
            return 0

        lax.fori_loop(k + 1, blocks, update, 0)
        return 0

    lax.fori_loop(UNROLLED, blocks, step, 0)
    for i in range(blocks):
        s = slice(i * 128, i * 128 + 128)
        lower = iota((128, PANEL), 1) < (i + 1) * 128
        high, low = split(jnp.where(lower, x_ref[s, :], 0.0))
        high_ref[s, :] = high
        low_ref[s, :] = low


COL_TILE = 256


def tile_kernel(
    where_ref, mine_ref, other_ref, c0_ref, c1_ref, c2_ref, c3_ref, high_ref, low_ref,
    schur_ref, factor_ref,
    g_ref, z_ref, row_sq_ref, panel_sq_ref, rows_ref, panel_ref, cols_ref
):
    my_col, my_row, owner = where_ref[2], where_ref[3], where_ref[4]
    step = pl.program_id(0)

    @pl.when(step == 0)
    def _():
        other = my_col + 1 - 2 * jnp.bitwise_and(my_col, 1)
        place(mine_ref, 0, my_col, rows_ref)
        place(other_ref, 0, other, rows_ref)
        place(mine_ref, 1, my_col, panel_ref)
        place(other_ref, 1, other, panel_ref)
        for i, c_ref in enumerate((c0_ref, c1_ref, c2_ref, c3_ref)):
            y = jnp.bitwise_and(my_row // 4 - HOPS[i], 3)
            for k, hop in enumerate(HOPS):
                r = y * 4 + jnp.bitwise_and(my_row - hop, 3)
                at = pl.ds(pl.multiple_of(r * GROUP, GROUP), GROUP)
                cols_ref[at, :] = c_ref[k * GROUP : (k + 1) * GROUP, :]
        rows, panel = rows_ref[...], panel_ref[...]
        rows_sq, panel_sq = sq_col(rows), sq_col(panel)
        row_sq_ref[...] = jnp.broadcast_to(rows_sq, (PANEL, 128))
        panel_sq_ref[...] = jnp.broadcast_to(panel_sq, (PANEL, 128))
        panel_row = as_row(panel_sq)
        ridge = jnp.where(my_row == owner, RIDGE, 0.0)
        for b in range(0, PANEL, BLOCK):
            s = slice(b, b + BLOCK)
            block = gram(rows, panel[s], rows_sq, panel_row[:, s])
            eye = iota((PANEL, BLOCK), 1) + b == iota((PANEL, BLOCK), 0)
            store_halves(g_ref, s, block + jnp.where(eye, ridge, 0.0))
        share = jnp.zeros((PANEL, GROUP), F32)
        for b in range(0, PANEL, BLOCK):
            s, upto = slice(b, b + BLOCK), slice(0, b + BLOCK)
            factor = stacked_dot(g_ref[:, upto], (high_ref[s, upto], low_ref[s, upto]), NT)
            store_halves(z_ref, s, factor)
            share = jnp.where(my_col == b // GROUP, factor[:, :GROUP], share)
            share = jnp.where(my_col == b // GROUP + 1, factor[:, GROUP:], share)
        factor_ref[...] = share
        for b in range(0, PANEL, BLOCK):
            s, upon = slice(b, b + BLOCK), slice(b, PANEL)
            z = stacked_dot(z_ref[:, upon], (high_ref[upon, s], low_ref[upon, s]), NN)
            store_halves(z_ref, s, z)

    cols = cols_ref[pl.ds(pl.multiple_of(step * COL_TILE, COL_TILE), COL_TILE), :]
    cols_sq = as_row(sq_col(cols))
    block = split(gram(panel_ref[...], cols, widen(panel_sq_ref[...]), cols_sq))
    tile = gram(rows_ref[...], cols, widen(row_sq_ref[...]), cols_sq)
    schur_ref[...] = tile - stacked_dot(z_ref[...], block, NN)

    @pl.when(step == owner // 2)
    def _():
        at = pl.ds(pl.multiple_of((owner % 2) * GROUP, GROUP), GROUP)
        of = pl.ds(pl.multiple_of(my_col * GROUP, GROUP), GROUP)
        z = z_ref[:PANEL, of].astype(F32) + z_ref[PANEL:, of].astype(F32)
        schur_ref[:, at] = schur_ref[:, at] - RIDGE * z

    @pl.when(step == my_row // 2)
    def _():
        at = pl.ds(pl.multiple_of((my_row % 2) * GROUP, GROUP), GROUP)
        of = pl.ds(pl.multiple_of(my_col * GROUP, GROUP), GROUP)
        eye = iota((GROUP, GROUP), 0) == iota((GROUP, GROUP), 1)
        schur_ref[of, at] = schur_ref[of, at] + jnp.where(eye, RIDGE, 0.0)


VMEM = pl.BlockSpec(memory_space=pltpu.VMEM)
SMEM = pl.BlockSpec(memory_space=pltpu.SMEM)


def call(kernel, out_shape, in_specs, scratch=(), **more):
    return pl.pallas_call(
        kernel,
        out_shape=out_shape,
        in_specs=in_specs,
        scratch_shapes=scratch,
        compiler_params=pltpu.CompilerParams(vmem_limit_bytes=40 << 20),
        **more,
    )


def body(descriptors, center_index, panel_index):
    my_row = lax.axis_index("row")
    my_col = lax.axis_index("col")
    owner = panel_index[0]
    flat = my_row * N_COL + my_col
    where = jnp.stack([flat, owner * N_COL, my_col, my_row, owner])
    index = center_index.reshape(DEVICES, GROUP)
    sent = call(
        send_kernel,
        jax.ShapeDtypeStruct((DEVICES * SLOTS, D), BF),
        [SMEM, VMEM, VMEM],
    )(where, index, descriptors)
    arrived = lax.all_to_all(sent, ("row", "col"), 0, 0, tiled=True)
    mine, own = call(
        take_kernel,
        (jax.ShapeDtypeStruct((2, GROUP, D), BF), jax.ShapeDtypeStruct((GROUP, D), BF)),
        [SMEM, VMEM, VMEM],
    )(where, index, arrived)
    near = [mine] + [
        lax.ppermute(mine, "col", [(i, (i // 2 + h) % 4 * 2 + i % 2) for i in range(N_COL)])
        for h in HOPS[1:]
    ]
    cols = [own] + [
        lax.ppermute(own, "row", [(i, i // 4 * 4 + (i + h) % 4) for i in range(N_ROW)])
        for h in HOPS[1:]
    ]
    near, cols = lax.optimization_barrier((near, cols))
    near = jnp.stack(near)
    cols = jnp.concatenate(cols, 0)
    other = lax.ppermute(near, "col", [(i, i ^ 1) for i in range(N_COL)])
    cols = [cols] + [
        lax.ppermute(cols, "row", [(i, (i // 4 + h) % 4 * 4 + i % 4) for i in range(N_ROW)])
        for h in HOPS[1:]
    ]
    square = jax.ShapeDtypeStruct((PANEL, PANEL), BF)
    pieces = pl.BlockSpec((4, 1, GROUP, D), lambda i: (0, 1, 0, 0))
    high, low = call(
        factor_kernel,
        (square, square),
        [SMEM, pieces, pieces],
        [pltpu.VMEM((PANEL, PANEL), F32), pltpu.VMEM((PANEL, D), BF)],
        grid=(1,),
        out_specs=(pl.BlockSpec((PANEL, PANEL), lambda i: (0, 0)),) * 2,
    )(where, near, other)
    width = N_ROW * GROUP
    halves = pltpu.VMEM((2 * PANEL, PANEL), BF)
    squares = pltpu.VMEM((PANEL, 128), F32)
    schur, factor = call(
        tile_kernel,
        (
            jax.ShapeDtypeStruct((PANEL, width), F32),
            jax.ShapeDtypeStruct((PANEL, GROUP), F32),
        ),
        [SMEM] + [VMEM] * 8,
        [halves, halves, squares, squares]
        + [pltpu.VMEM((PANEL, D), BF), pltpu.VMEM((PANEL, D), BF), pltpu.VMEM((width, D), BF)],
        grid=(width // COL_TILE,),
        out_specs=(
            pl.BlockSpec((PANEL, COL_TILE), lambda i: (0, i)),
            pl.BlockSpec((PANEL, GROUP), lambda i: (0, 0)),
        ),
    )(where, near, other, *cols, high, low)
    return schur, factor


def solution(mesh):
    return jax.shard_map(
        body,
        mesh=mesh,
        in_specs=(P(("row", "col"), None), P(), P()),
        out_specs=(P("row", "col"), P("row", "col")),
        check_vma=False,
    )
```
